256 devices in a mesh: outer: 16 (over z_hi, x), inner: 16 (over y, z_lo, core).
Axes of the slice: x: 4, y: 4, z: 8 (z_hi: 4, z_lo: 2; z = z_hi * 2 + z_lo), core: 2. Of those that a mesh axis runs over, the one named last changes fastest.
Arguments:
- queries: bfloat16 [65536, 1024], P(('outer', 'inner')), may hold values from -48 to 48
- keys: bfloat16 [65536, 128], P(('outer', 'inner')), may hold values from -4 to 4
- values: bfloat16 [65536, 128], P(('outer', 'inner')), may hold values from -6 to 6
- reflect: bfloat16 [65536, 128], P(('outer', 'inner')), may hold values from -6 to 6
- reflect_logit: float32 [65536], P(('outer', 'inner')), may hold values from -8 to 8
- doc_of_block: int32 [256], replicated, may hold values from 0 to 15, never falling along the last dimension, each value on 1 to 32 neighbouring positions
Outputs:
- attended: bfloat16 [65536, 1024], P(('outer', 'inner'))
The draws below stay inside these ranges and needn't reach their ends.
Inputs may be any that keep to these rules, and one draw needn't show every extreme that they name: `doc_of_block`: document numbers never fall along the blocks; every document covers 1 to 32 consecutive blocks, and one covers exactly 32.
All inputs are finite; a program needn't handle non-finite values.
Results may differ from the reference program's by a relative error of at most 0.017.
Values may be sent and summed in bfloat16 or wider, within the bound.
A program may use at most 64 MiB of HBM per device.

```python
import math
import jax
import jax.numpy as jnp
import numpy as np
from jax import lax

HEAD = 128
QHEADS = 8
TOK_DEV = 256
BLOCKS = 256
TOKENS = 65536
MOST = 32


def joint_draw(key):
    query_seed = jax.random.fold_in(key, 101)
    key_seed = jax.random.fold_in(key, 102)
    mirror_seed = jax.random.fold_in(key, 103)
    key_rows = jnp.clip(jax.random.normal(key_seed, (TOKENS, HEAD), jnp.float32), -4.0, 4.0)
    query_rows = jnp.clip(jax.random.normal(query_seed, (TOKENS, QHEADS, HEAD), jnp.float32), -6.0, 6.0)
    reflect_rows = jnp.clip(jax.random.normal(mirror_seed, (TOKENS, HEAD), jnp.float32), -6.0, 6.0)
    return (query_rows.reshape(TOKENS, QHEADS * HEAD), key_rows, reflect_rows)


def draw_queries(key, part):
    return joint_draw(key)[0].astype(jnp.bfloat16)


def draw_keys(key, part):
    return joint_draw(key)[1].astype(jnp.bfloat16)


def draw_reflect(key, part):
    return joint_draw(key)[2].astype(jnp.bfloat16)


def draw_reflect_logit(key, part):
    size_seed = jax.random.fold_in(key, 201)
    sign_seed = jax.random.fold_in(key, 202)
    magnitude = jax.random.uniform(size_seed, (TOKENS,), jnp.float32, 4.0, 8.0)
    flips = jax.random.bernoulli(sign_seed, 0.5, (TOKENS,))
    return jnp.where(flips, magnitude, -magnitude).astype(jnp.float32)


def shard_levels(own_key, shape, shards, least, largest):
    factor_of, own = 1.0, jax.random.fold_in(own_key, 6)
    for dim, parts in shards:
        heights = jnp.exp(jax.random.uniform(jax.random.fold_in(own, dim), (parts,), jnp.float32, least / len(shards), largest / len(shards)))
        factor_of = factor_of * jnp.repeat(heights, shape[dim] // parts).reshape([-1 if axis == dim else 1 for axis in range(len(shape))])
    return factor_of


def length_profile(amount, total, most, skew):
    loads = [(1 << 20) // math.isqrt(grade ** skew) + 1 for grade in range(2, amount + 1)]
    spare, given = total - most - (amount - 1), [1] * (amount - 1)
    while spare > 0:
        candidates = [i for i in range(amount - 1) if given[i] < most]
        mass, left = sum([loads[i] for i in candidates]), spare
        for i in candidates:
            addition = min(most - given[i], max(1, left * loads[i] // mass), spare)
            given[i] = given[i] + addition
            spare = spare - addition
    return np.array([most] + given)


def ragged_sizes(stream_key, amount, total, most, lean):
    if amount == 2:
        one = jax.random.randint(stream_key, (), max(1, total - most), min(most, total - 1) + 1)
        return jnp.stack([one, total - one])
    tallies = jnp.asarray(length_profile(amount, total, most, lean), jnp.int32)
    pairs = (amount - 1) // 2
    source_of, sink = tallies[1:1 + 2 * pairs:2], tallies[2:2 + 2 * pairs:2]
    margin = jnp.minimum(source_of - 1, most - sink)
    moved = jax.random.randint(jax.random.fold_in(stream_key, 1), (pairs,), 0, 1 << 20) % (margin + 1)
    tallies = tallies.at[1:1 + 2 * pairs:2].set(source_of - moved).at[2:2 + 2 * pairs:2].set(sink + moved)
    return tallies[jax.random.permutation(jax.random.fold_in(stream_key, 2), amount)]


def normal_values(own_key, shape, deviation, most, split=(), kind=jnp.bfloat16):
    entries = deviation * jax.random.normal(own_key, shape, jnp.float32)
    if split:
        entries = entries * shard_levels(own_key, shape, split, -0.22, 0.18)
    return jnp.clip(entries, -most, most).astype(kind)


def setup_inputs(seed: int = 0) -> dict:
    streams_of = jax.random.split(jax.random.key(seed), 7)
    queries = draw_queries(jax.random.fold_in(streams_of[6], 71), 0)
    keys = draw_keys(jax.random.fold_in(streams_of[6], 71), 0)
    values = normal_values(streams_of[2], (TOKENS, HEAD), 1.0, 6.0, ((0, 256),))
    reflect = draw_reflect(jax.random.fold_in(streams_of[6], 71), 0)
    reflect_logit = draw_reflect_logit(jax.random.fold_in(streams_of[6], 71), 0)
    doc_of_block = jnp.searchsorted(jnp.cumsum(ragged_sizes(streams_of[5], 16, BLOCKS, MOST, 1)), jnp.arange(BLOCKS), side="right").astype(jnp.int32)
    return {"queries": queries, "keys": keys, "values": values, "reflect": reflect, "reflect_logit": reflect_logit, "doc_of_block": doc_of_block}


def matmul(left_side, right_side):
    return jnp.dot(left_side, right_side, precision=lax.Precision.HIGHEST, preferred_element_type=jnp.float32)

def apply_map(vectors, matrix):
    return lax.dot_general(vectors, matrix, (((1,), (1,)), ((), ())), precision=lax.Precision.HIGHEST, preferred_element_type=jnp.float32)

def unit_inverse(strict_part):
    length = strict_part.shape[0]
    identity = jnp.eye(length, dtype=jnp.float32)
    result = identity - strict_part
    power = strict_part
    reach = 2
    while reach < length:
        power = matmul(power, power)
        result = matmul(result, identity + power)
        reach = reach * 2
    return result

def prepare(queries, keys, reflect, reflect_logit):
    length = keys.shape[0]
    head_size = keys.shape[1]
    head_count = queries.shape[1] // head_size
    direction = reflect.astype(jnp.float32)
    direction = direction * lax.rsqrt(lax.optimization_barrier(jnp.sum(direction * direction, axis=1, keepdims=True)) + 1e-06)
    strength = 2.0 * jax.nn.sigmoid(reflect_logit.astype(jnp.float32))
    scaled_dirs = direction * strength[:, None]
    places = jnp.arange(length)
    strictly = places[:, None] > places[None, :]
    intersection = apply_map(direction, direction)
    lower_inverse = unit_inverse(jnp.where(strictly, intersection, 0.0) * strength[None, :])
    upper_inverse = unit_inverse(jnp.where(strictly.T, intersection, 0.0) * strength[None, :])
    key_float = keys.astype(jnp.float32)
    updates = matmul(lower_inverse, jnp.where(strictly, apply_map(direction, key_float), 0.0))
    key_end = key_float - matmul(updates.T, scaled_dirs)
    reflected = matmul(lower_inverse, direction)
    transit = jnp.eye(head_size, dtype=jnp.float32) - matmul(scaled_dirs.T, reflected)
    query_rows = queries.reshape(length, head_count, head_size).transpose(1, 0, 2).reshape(head_count * length, head_size)
    query_float = query_rows.astype(jnp.float32)
    facing = apply_map(query_float, direction)
    query_places = jnp.tile(places, head_count)
    visible = places[None, :] <= query_places[:, None]
    solved = matmul(upper_inverse, jnp.where(visible.T, facing.T, 0.0))
    query_turned = (query_float - matmul(solved.T, scaled_dirs)).astype(jnp.bfloat16)
    direct = lax.dot_general(query_rows, keys, (((1,), (1,)), ((), ())), preferred_element_type=jnp.float32)
    inside = (direct - matmul(jnp.where(visible, facing, 0.0) * strength[None, :], updates)) * head_size ** (-0.5)
    inside = jnp.where(visible, inside, -1e+30)
    return (query_turned, inside, key_end, transit)

def reference(queries, keys, values, reflect, reflect_logit, doc_of_block):
    head_size = keys.shape[1]
    head_count = queries.shape[1] // head_size
    stack_depth = MOST - 1

    def per_block(stacks, inputs):
        stack_keys, stack_values, stack_docs = stacks
        query_block, key_block, value_block, reflect_block, logit_block, doc_now = inputs
        query_turned, inside, key_end, transit = prepare(query_block, key_block, reflect_block, logit_block)
        flat_keys = stack_keys.reshape(stack_depth * TOK_DEV, head_size)
        remote = lax.dot_general(query_turned, flat_keys.astype(jnp.bfloat16), (((1,), (1,)), ((), ())), preferred_element_type=jnp.float32) * head_size ** (-0.5)
        allowed = jnp.repeat(stack_docs == doc_now, TOK_DEV)
        remote = jnp.where(allowed[None, :], remote, -1e+30)
        row_peak = jnp.maximum(lax.optimization_barrier(jnp.max(inside, axis=1, keepdims=True)), lax.optimization_barrier(jnp.max(remote, axis=1, keepdims=True)))
        near_w = jnp.exp(inside - row_peak)
        far_w = jnp.exp(remote - row_peak)
        weight_sum = lax.optimization_barrier(jnp.sum(near_w, axis=1, keepdims=True)) + lax.optimization_barrier(jnp.sum(far_w, axis=1, keepdims=True))
        weighted = jnp.dot(near_w.astype(jnp.bfloat16), value_block, preferred_element_type=jnp.float32)
        weighted = weighted + jnp.dot(far_w.astype(jnp.bfloat16), stack_values.reshape(stack_depth * TOK_DEV, head_size), preferred_element_type=jnp.float32)
        result = (weighted / weight_sum).reshape(head_count, TOK_DEV, head_size).transpose(1, 0, 2)
        attended_block = result.reshape(TOK_DEV, head_count * head_size).astype(jnp.bfloat16)
        carried = apply_map(flat_keys, transit).reshape(stack_depth, TOK_DEV, head_size)
        stack_keys = jnp.concatenate([carried[1:], key_end[None]], axis=0)
        stack_values = jnp.concatenate([stack_values[1:], value_block[None]], axis=0)
        stack_docs = jnp.concatenate([stack_docs[1:], doc_now[None]], axis=0)
        return ((stack_keys, stack_values, stack_docs), attended_block)
    opening = (jnp.zeros((stack_depth, TOK_DEV, head_size), jnp.float32), jnp.zeros((stack_depth, TOK_DEV, head_size), jnp.bfloat16), jnp.full((stack_depth,), -1, jnp.int32))
    inputs = (queries.reshape(BLOCKS, TOK_DEV, head_count * head_size), keys.reshape(BLOCKS, TOK_DEV, head_size), values.reshape(BLOCKS, TOK_DEV, head_size), reflect.reshape(BLOCKS, TOK_DEV, head_size), reflect_logit.reshape(BLOCKS, TOK_DEV), doc_of_block.astype(jnp.int32))
    final_stacks, blocks_out = lax.scan(per_block, opening, inputs)
    return blocks_out.reshape(TOKENS, head_count * head_size)
```

```python
import functools
import math

import jax
import jax.numpy as jnp
from jax import lax
from jax.experimental import pallas as pl
from jax.experimental.pallas import tpu as pltpu
from jax.sharding import PartitionSpec as P

F32 = jnp.float32
BF = jnp.bfloat16
MESH = pl.DeviceIdType.MESH
NEG = -1e30
TOK = 256
HEAD = 128
HEADS = 8
INNER = 16
SLOTS = 48
CHUNK = 4
SOURCES = 32
SCALE = math.log2(math.e) / math.sqrt(HEAD)


def nn(a, b):
    return jnp.dot(a, b, preferred_element_type=F32)


def nt(a, b):
    return lax.dot_general(a, b, (((1,), (1,)), ((), ())), preferred_element_type=F32)


def split(x):
    hi = x.astype(BF)
    return hi, (x - hi.astype(F32)).astype(BF)


def mm3(a, b):
    ah, al = split(a)
    bh, bl = split(b)
    return nn(ah, bh) + (nn(ah, bl) + nn(al, bh))


def inverse_pair(first, second):
    half = first.shape[0]
    eye = (
        lax.broadcasted_iota(jnp.int32, (half, half), 0)
        == lax.broadcasted_iota(jnp.int32, (half, half), 1)
    ).astype(F32)
    powers = [-first, -second]
    results = [eye + p for p in powers]
    powers = [mm3(p, p) for p in powers]
    reach = 4
    while reach < half:
        stacked = [jnp.concatenate([r, p], axis=0) for r, p in zip(results, powers)]
        grown = [mm3(s, p) for s, p in zip(stacked, powers)]
        results = [r + g[:half] for r, g in zip(results, grown)]
        powers = [g[half:] for g in grown]
        reach *= 2
    return [r + mm3(r, p) for r, p in zip(results, powers)]


def kernel(
    q_ref, k_ref, v_ref, w_ref, logit_ref, doc_ref, out_ref,
    vbuf, tkbuf, qext, keyst, accs, peaks, chain,
    v_recv, tk_recv, v_send, tk_send, local_sem,
):
    outer = lax.axis_index("outer")
    inner = lax.axis_index("inner")
    groups = lax.axis_size("outer")
    block = outer * INNER + inner
    y = inner // 4
    zl = (inner // 2) % 2
    core = inner % 2

    def at_inner(ny, nz, nc):
        return ny * 4 + nz * 2 + nc

    z_peer = (outer, at_inner(y, 1 - zl, core))
    core_peer = (outer, at_inner(y, zl, 1 - core))
    y_peers = [(outer, at_inner((y + dy) % 4, zl, core)) for dy in (1, 2, 3)]
    y_from = [(y + 4 - dy) % 4 for dy in (1, 2, 3)]
    x_peers = [((outer + d) % groups, inner) for d in (1, 2)]
    x_back = [((outer + groups - d) % groups, inner) for d in (1, 2)]

    barrier = pltpu.get_barrier_semaphore()
    everyone = [z_peer, core_peer] + y_peers + x_peers + x_back
    for peer in everyone:
        pl.semaphore_signal(barrier, inc=1, device_id=peer, device_id_type=MESH)

    own = pltpu.make_async_copy(v_ref, vbuf.at[32 + inner], local_sem)
    own.start()
    own.wait()
    pl.semaphore_wait(barrier, len(everyone))

    def slot_of(source, receiver, step):
        later = jnp.where(source > receiver, 1, 0)
        return 32 - 16 * (later + step) + source

    class Mover:
        def __init__(self, buf, send, recv):
            self.buf, self.send, self.recv, self.sent = buf, send, recv, []

        def copy(self, source, target, peer):
            n = len(self.sent)
            made = pltpu.make_async_remote_copy(
                src_ref=self.buf.at[source],
                dst_ref=self.buf.at[target],
                send_sem=self.send.at[n],
                recv_sem=self.recv.at[target],
                device_id=peer,
                device_id_type=MESH,
            )
            made.start()
            self.sent.append(made)

        def arrived(self, slot):
            pltpu.make_async_remote_copy(
                src_ref=self.buf.at[slot],
                dst_ref=self.buf.at[slot],
                send_sem=self.send.at[0],
                recv_sem=self.recv.at[slot],
                device_id=core_peer,
                device_id_type=MESH,
            ).wait_recv()

        def drain(self):
            for made in self.sent:
                made.wait_send()

        def x_start(self):
            self.copy(32 + inner, 16 + inner, x_peers[0])
            self.copy(32 + inner, inner, x_peers[1])

        def x_wait(self):
            self.arrived(16 + inner)
            self.arrived(inner)

        def y_start(self, nz):
            source = at_inner(y, nz, core)
            for peer in y_peers:
                for step in (0, 1):
                    slot = slot_of(source, at_inner(peer[1] // 4, nz, core), step)
                    self.copy(slot, slot, peer)

        def y_slots(self, nz):
            return [
                slot_of(at_inner(ny, nz, core), inner, step) for ny in y_from for step in (0, 1)
            ]

        def core_start(self):
            for place in range(8):
                source = place * 2 + core
                for step in (0, 1):
                    slot = slot_of(source, core_peer[1], step)
                    self.copy(slot, slot, core_peer)

        def core_wait(self):
            for place in range(8):
                source = place * 2 + 1 - core
                for step in (0, 1):
                    self.arrived(slot_of(source, inner, step))

    values = Mover(vbuf, v_send, v_recv)
    maps = Mover(tkbuf, tk_send, tk_recv)

    values.x_start()

    w0 = w_ref[...]
    key_rows = k_ref[...]
    rows = lax.broadcasted_iota(jnp.int32, (TOK, TOK), 0)
    cols = lax.broadcasted_iota(jnp.int32, (TOK, TOK), 1)
    eye = rows == cols
    gram = nt(w0, w0)
    diagonal = jnp.where(eye, gram, 0.0)
    norm_col = lax.rsqrt(jnp.sum(diagonal, axis=1, keepdims=True) + 1e-6)
    norm_row = lax.rsqrt(jnp.sum(diagonal, axis=0, keepdims=True) + 1e-6)
    beta_row = 2.0 / (1.0 + jnp.exp(-logit_ref[...]))
    beta_col = jnp.sum(
        jnp.where(eye, jnp.broadcast_to(beta_row, (TOK, TOK)), 0.0), axis=1, keepdims=True
    )
    reach_row = norm_row * beta_row
    below = rows > cols
    strict = jnp.where(below, gram * norm_col * reach_row, 0.0)
    cross = jnp.where(below, nt(w0, key_rows) * norm_col, 0.0)
    unit = w0.astype(F32) * norm_col
    right = jnp.concatenate([unit, cross], axis=1)
    half = TOK // 2
    inv_first, inv_second = inverse_pair(strict[:half, :half], strict[half:, half:])

    values.x_wait()
    for slot in (32 + inner, 16 + inner, inner):
        values.copy(slot, slot, z_peer)
    values.y_start(zl)

    solved_first = mm3(inv_first, right[:half])
    solved_second = mm3(inv_second, right[half:] - mm3(strict[half:, :half], solved_first))
    solved = jnp.concatenate([solved_first, solved_second], axis=0)
    scaled_t = (unit * beta_col).T
    key_t = key_rows.astype(F32).T
    eye_head = (
        lax.broadcasted_iota(jnp.int32, (HEAD, HEAD), 0)
        == lax.broadcasted_iota(jnp.int32, (HEAD, HEAD), 1)
    ).astype(F32)
    own_map = jnp.concatenate([eye_head, key_t], axis=1) - mm3(scaled_t, solved)
    tkbuf[32 + inner] = own_map.astype(BF)
    solved_hi, solved_lo = split(solved)

    partner = at_inner(y, 1 - zl, core)
    for slot in (32 + partner, 16 + partner, partner):
        values.arrived(slot)
    values.y_start(1 - zl)

    maps.x_start()

    ones = jnp.ones((TOK, HEAD), BF)
    visible = rows >= cols
    lanes = lax.broadcasted_iota(jnp.int32, (TOK, HEAD), 1)
    first_lane = jnp.where(lanes == 0, 1.0, 0.0).astype(BF)

    def prepare_head(h, carry):
        q = q_ref[:, pl.ds(pl.multiple_of(h * HEAD, HEAD), HEAD)]
        facing = jnp.where(visible, nt(q, w0) * reach_row, 0.0)
        face_hi = facing.astype(BF)
        moved = nn(face_hi, solved_hi) + nn(face_hi, solved_lo)
        turned = (q.astype(F32) - moved[:, :HEAD]) * SCALE
        qext[h] = jnp.concatenate([turned.astype(BF), first_lane], axis=1)
        inside = (nt(q, key_rows) - moved[:, HEAD:]) * SCALE
        inside = jnp.where(visible, inside, NEG)
        peak = jnp.max(inside, axis=1, keepdims=True)
        weights = jnp.exp2(inside - peak).astype(BF)
        accs[h] = nn(weights, jnp.concatenate([v_ref[...], ones], axis=1))
        peaks[h] = jnp.broadcast_to(peak, (TOK, HEAD))
        return carry

    lax.fori_loop(0, HEADS // 2, prepare_head, 0)
    maps.x_wait()
    maps.y_start(zl)
    lax.fori_loop(HEADS // 2, HEADS, prepare_head, 0)

    for slot in maps.y_slots(zl):
        maps.arrived(slot)
    for ny in range(4):
        source = at_inner(ny, zl, core)
        for step in (0, 1):
            slot = slot_of(source, z_peer[1], step)
            maps.copy(slot, slot, z_peer)
    for nz in (zl, 1 - zl):
        for slot in values.y_slots(nz):
            values.arrived(slot)
    values.core_start()
    for ny in range(4):
        for step in (0, 1):
            maps.arrived(slot_of(at_inner(ny, 1 - zl, core), inner, step))
    maps.core_start()
    values.core_wait()
    maps.core_wait()

    keyst[128:, :] = jnp.zeros((128, SOURCES * TOK), BF)
    tile_row = lax.broadcasted_iota(jnp.int32, (16, TOK), 0)
    chain[...] = eye_head
    own_doc = doc_ref[block]

    def carry_keys(index, carry):
        distance = jnp.minimum(index + 1, SOURCES - 1)
        hi, lo = split(chain[...])
        both = tkbuf[32 + inner - distance]
        moved = nn(hi, both) + nn(lo, both)
        chain[...] = moved[:, :HEAD]
        at = pl.ds(pl.multiple_of(index * TOK, TOK), TOK)
        keyst[:HEAD, at] = moved[:, HEAD:].astype(BF)
        source = block - distance
        wanted = (
            (source >= 0) & (index < SOURCES - 1) & (doc_ref[jnp.maximum(source, 0)] == own_doc)
        )
        bias = jnp.where(wanted, 0.0, NEG)
        keyst[128:144, at] = jnp.where(tile_row == 0, bias, 0.0).astype(BF)
        return carry

    lax.fori_loop(0, SOURCES, carry_keys, 0)

    def absorb(step, carry):
        chunk = step // HEADS
        h = step % HEADS
        at = pl.ds(pl.multiple_of(chunk * (CHUNK * TOK), TOK), CHUNK * TOK)
        scores = nn(qext[h], keyst[:, at])
        old = peaks[h]
        peak = jnp.maximum(old, jnp.max(scores, axis=1, keepdims=True))
        factor = jnp.exp2(old - peak)
        total = accs[h] * jnp.concatenate([factor, factor], axis=1)
        for part in range(CHUNK):
            piece = scores[:, part * TOK : (part + 1) * TOK]
            weights = jnp.exp2(piece - jnp.concatenate([peak, peak], axis=1)).astype(BF)
            distance = jnp.minimum(chunk * CHUNK + part + 1, SOURCES - 1)
            total += nn(weights, jnp.concatenate([vbuf[32 + inner - distance], ones], axis=1))
        accs[h] = total
        peaks[h] = peak
        return carry

    lax.fori_loop(0, SOURCES // CHUNK * HEADS, absorb, 0)

    def finish(h, carry):
        total = accs[h]
        out_ref[:, pl.ds(pl.multiple_of(h * HEAD, HEAD), HEAD)] = (
            total[:, :HEAD] / total[:, HEAD:]
        ).astype(BF)
        return carry

    lax.fori_loop(0, HEADS, finish, 0)
    values.drain()
    maps.drain()


def local(queries, keys, values, reflect, reflect_logit, doc_of_block):
    vmem = pl.BlockSpec(memory_space=pltpu.VMEM)
    return pl.pallas_call(
        kernel,
        out_shape=jax.ShapeDtypeStruct(queries.shape, BF),
        in_specs=[vmem] * 5 + [pl.BlockSpec(memory_space=pltpu.SMEM)],
        out_specs=vmem,
        scratch_shapes=[
            pltpu.VMEM((SLOTS, TOK, HEAD), BF),
            pltpu.VMEM((SLOTS, HEAD, HEAD + TOK), BF),
            pltpu.VMEM((HEADS, TOK, 2 * HEAD), BF),
            pltpu.VMEM((2 * HEAD, SOURCES * TOK), BF),
            pltpu.VMEM((HEADS, TOK, 2 * HEAD), F32),
            pltpu.VMEM((HEADS, TOK, HEAD), F32),
            pltpu.VMEM((HEAD, HEAD), F32),
            pltpu.SemaphoreType.DMA((SLOTS,)),
            pltpu.SemaphoreType.DMA((SLOTS,)),
            pltpu.SemaphoreType.DMA((33,)),
            pltpu.SemaphoreType.DMA((32,)),
            pltpu.SemaphoreType.DMA,
        ],
        compiler_params=pltpu.CompilerParams(
            collective_id=0, has_side_effects=True, vmem_limit_bytes=48 * 1024 * 1024
        ),
    )(queries, keys, values, reflect, reflect_logit.reshape(1, TOK), doc_of_block)


def solution(mesh):
    placed = (
        P(("outer", "inner"), None),
        P(("outer", "inner"), None),
        P(("outer", "inner"), None),
        P(("outer", "inner"), None),
        P(("outer", "inner")),
        P(),
    )
    return jax.shard_map(
        local, mesh=mesh, in_specs=placed, out_specs=P(("outer", "inner"), None), check_vma=False
    )
```

```python
import functools
import math

import jax
import jax.numpy as jnp
from jax import lax
from jax.experimental import pallas as pl
from jax.experimental.pallas import tpu as pltpu
from jax.sharding import PartitionSpec as P

F32 = jnp.float32
BF = jnp.bfloat16
MESH = pl.DeviceIdType.MESH
NEG = -1e30
TOK = 256
HEAD = 128
HEADS = 8
INNER = 16
SLOTS = 48
CHUNK = 4
SOURCES = 32
PAIRS = 4
TAGS = [("x", 0, 0)] + [(k, age, 0) for age in range(3) for k in "zy"] + [("y", age, 1) for age in range(3)]
SENDS = 23
AHEAD = 2
SCALE = math.log2(math.e) / math.sqrt(HEAD)


def nn(a, b):
    return jnp.dot(a, b, preferred_element_type=F32)


def nt(a, b):
    return lax.dot_general(a, b, (((1,), (1,)), ((), ())), preferred_element_type=F32)


def split(x):
    hi = x.astype(BF)
    return hi, (x - hi.astype(F32)).astype(BF)


def mm3(a, b):
    ah, al = split(a)
    bh, bl = split(b)
    return nn(ah, bh) + (nn(ah, bl) + nn(al, bh))


def inverse_pair(first, second):
    half = first.shape[0]
    eye = (
        lax.broadcasted_iota(jnp.int32, (half, half), 0)
        == lax.broadcasted_iota(jnp.int32, (half, half), 1)
    ).astype(F32)
    powers = [-first, -second]
    results = [eye + p for p in powers]
    powers = [mm3(p, p) for p in powers]
    reach = 4
    while reach < half:
        stacked = [jnp.concatenate([r, p], axis=0) for r, p in zip(results, powers)]
        grown = [mm3(s, p) for s, p in zip(stacked, powers)]
        results = [r + g[:half] for r, g in zip(results, grown)]
        powers = [g[half:] for g in grown]
        reach *= 2
    return [r + mm3(r, p) for r, p in zip(results, powers)]


def kernel(
    q_ref, k_ref, v_ref, w_ref, logit_ref, doc_ref, out_ref,
    vbuf, tkbuf, qext, keyst, vext, accs, peaks, chain, score_a, score_b, high_a, high_b,
    v_recv, tk_recv, v_send, tk_send, local_sem,
):
    outer = lax.axis_index("outer")
    inner = lax.axis_index("inner")
    groups = lax.axis_size("outer")
    block = outer * INNER + inner
    y = inner // 4
    zl = (inner // 2) % 2
    core = inner % 2

    def at_inner(ny, nz, nc):
        return ny * 4 + nz * 2 + nc

    z_peer = (outer, at_inner(y, 1 - zl, core))
    core_peer = (outer, at_inner(y, zl, 1 - core))
    y_peers = [(outer, at_inner((y + dy) % 4, zl, core)) for dy in (1, 2, 3)]
    partner = at_inner(y, 1 - zl, core)
    x_peers = [((outer + d) % groups, inner) for d in (1, 2)]
    x_back = [((outer + groups - d) % groups, inner) for d in (1, 2)]

    barrier = pltpu.get_barrier_semaphore()
    everyone = [z_peer, core_peer] + y_peers + x_peers + x_back
    for peer in everyone:
        pl.semaphore_signal(barrier, inc=1, device_id=peer, device_id_type=MESH)

    own = pltpu.make_async_copy(v_ref, vbuf.at[32 + inner], local_sem)
    own.start()
    own.wait()
    pl.semaphore_wait(barrier, len(everyone))

    def guarded(when, action):
        if when is None:
            action()
        else:
            pl.when(when)(action)

    class Mover:
        def __init__(self, buf, send, recv):
            self.buf, self.send, self.recv = buf, send, recv

        def copies(self, tag):
            kind, age, side = tag
            if kind == "x":
                moves = [(32 + inner, 16 + inner, x_peers[0], None), (32 + inner, inner, x_peers[1], None)]
            else:
                source = inner if side == 0 else partner
                slot = 32 - 16 * age + source
                if kind == "z":
                    moves = [(slot, slot, z_peer, None)]
                else:
                    moves = [
                        (slot, slot, peer, (y + dy < 4, None, y + dy >= 4)[age])
                        for dy, peer in zip((1, 2, 3), y_peers)
                    ]
            first = sum(3 if t[0] == "y" else 2 if t[0] == "x" else 1 for t in TAGS[: TAGS.index(tag)])
            for number, (start, target, peer, when) in enumerate(moves):
                made = pltpu.make_async_remote_copy(
                    src_ref=self.buf.at[start],
                    dst_ref=self.buf.at[target],
                    send_sem=self.send.at[first + number],
                    recv_sem=self.recv.at[target],
                    device_id=peer,
                    device_id_type=MESH,
                )
                yield when, made

        def begin_copies(self, *tag):
            for when, made in self.copies(tag):
                guarded(when, made.start)

        def across(self, slot, number):
            return pltpu.make_async_remote_copy(
                src_ref=self.buf.at[slot],
                dst_ref=self.buf.at[slot],
                send_sem=self.send.at[SENDS + number],
                recv_sem=self.recv.at[slot],
                device_id=core_peer,
                device_id_type=MESH,
            )

        def arrived(self, slot):
            self.across(slot, 0).wait_recv()

        def drain(self):
            for tag in TAGS:
                for when, made in self.copies(tag):
                    guarded(when, made.wait_send)

        def begin(self):
            self.begin_copies("x", 0, 0)
            self.begin_copies("z", 0, 0)
            guarded(core == 0, self.across(32 + inner, 0).start)
            self.begin_copies("y", 0, 0)

        def after_z(self, age):
            self.arrived(32 - 16 * age + partner)
            self.begin_copies("y", age, 1)

        def after_x(self, age):
            self.arrived(32 - 16 * age + inner)
            self.begin_copies("z", age, 0)
            self.begin_copies("y", age, 0)

    values = Mover(vbuf, v_send, v_recv)
    maps = Mover(tkbuf, tk_send, tk_recv)

    values.begin()

    w0 = w_ref[...]
    key_rows = k_ref[...]
    rows = lax.broadcasted_iota(jnp.int32, (TOK, TOK), 0)
    cols = lax.broadcasted_iota(jnp.int32, (TOK, TOK), 1)
    eye = rows == cols
    gram = nt(w0, w0)
    diagonal = jnp.where(eye, gram, 0.0)
    norm_col = lax.rsqrt(jnp.sum(diagonal, axis=1, keepdims=True) + 1e-6)
    norm_row = lax.rsqrt(jnp.sum(diagonal, axis=0, keepdims=True) + 1e-6)
    beta_row = 2.0 / (1.0 + jnp.exp(-logit_ref[...]))
    beta_col = jnp.sum(
        jnp.where(eye, jnp.broadcast_to(beta_row, (TOK, TOK)), 0.0), axis=1, keepdims=True
    )
    reach_row = norm_row * beta_row
    below = rows > cols
    strict = jnp.where(below, gram * norm_col * reach_row, 0.0)
    cross = jnp.where(below, nt(w0, key_rows) * norm_col, 0.0)
    unit = w0.astype(F32) * norm_col
    right = jnp.concatenate([unit, cross], axis=1)
    half = TOK // 2
    values.after_z(0)
    values.after_x(1)
    inv_first, inv_second = inverse_pair(strict[:half, :half], strict[half:, half:])
    values.after_z(1)
    values.after_x(2)
    solved_first = mm3(inv_first, right[:half])
    solved_second = mm3(inv_second, right[half:] - mm3(strict[half:, :half], solved_first))
    solved = jnp.concatenate([solved_first, solved_second], axis=0)
    scaled_t = (unit * beta_col).T
    key_t = key_rows.astype(F32).T
    eye_head = (
        lax.broadcasted_iota(jnp.int32, (HEAD, HEAD), 0)
        == lax.broadcasted_iota(jnp.int32, (HEAD, HEAD), 1)
    ).astype(F32)
    own_map = jnp.concatenate([eye_head, key_t], axis=1) - mm3(scaled_t, solved)
    tkbuf[32 + inner] = own_map.astype(BF)
    solved_hi, solved_lo = split(solved)

    maps.begin()
    values.after_z(2)

    ones = jnp.ones((TOK, HEAD), BF)
    visible = rows >= cols
    lanes = lax.broadcasted_iota(jnp.int32, (TOK, HEAD), 1)
    first_lane = jnp.where(lanes == 0, 1.0, 0.0).astype(BF)

    own_values = jnp.concatenate([v_ref[...], ones], axis=1)

    def prepare_head(h, g, at):
        q = q_ref[:, pl.ds(pl.multiple_of(h * HEAD, HEAD), HEAD)]
        facing = jnp.where(visible, nt(q, w0) * reach_row, 0.0)
        face_hi = facing.astype(BF)
        moved = nn(face_hi, solved_hi) + nn(face_hi, solved_lo)
        turned = (q.astype(F32) - moved[:, :HEAD]) * SCALE
        qext[g, at, :] = jnp.concatenate([turned.astype(BF), first_lane], axis=1)
        inside = (nt(q, key_rows) - moved[:, HEAD:]) * SCALE
        inside = jnp.where(visible, inside, NEG)
        peak = jnp.max(inside, axis=1, keepdims=True)
        weights = jnp.exp2(inside - peak).astype(BF)
        accs[g, at, :] = nn(weights, own_values)
        peaks[g, at, :] = jnp.broadcast_to(peak, (TOK, HEAD))

    def prepare_pair(g, carry):
        for half_pair in range(2):
            prepare_head(g * 2 + half_pair, g, slice(half_pair * TOK, half_pair * TOK + TOK))
        pl.when(g == 0)(lambda: maps.after_z(0))
        pl.when(g == 1)(lambda: maps.after_x(1))
        pl.when(g == 2)(lambda: maps.after_z(1))
        return carry

    lax.fori_loop(0, PAIRS, prepare_pair, 0)
    maps.after_x(2)
    maps.after_z(2)

    def forward(e):
        slot = 32 + inner - 2 * e

        @pl.when((slot % INNER // 4 != y) & (e < 16))
        def _():
            values.arrived(slot)
            maps.arrived(slot)

        @pl.when((e < 16) | (core == 1))
        def _():
            values.across(slot, e).start()
            maps.across(slot, e).start()

    def forward_step(e, carry):
        forward(e)
        return carry

    lax.fori_loop(1, AHEAD + 3, forward_step, 0)

    keyst[128:, :] = jnp.zeros((128, keyst.shape[1]), BF)
    tile_row = lax.broadcasted_iota(jnp.int32, (16, TOK), 0)
    chain[...] = eye_head
    own_doc = doc_ref[block]

    def carry_keys(index):
        distance = jnp.minimum(index + 1, SOURCES - 1)
        hi, lo = split(chain[...])
        both = tkbuf[32 + inner - distance]
        moved = nn(hi, both) + nn(lo, both)
        chain[...] = moved[:, :HEAD]
        at = pl.ds(pl.multiple_of(index * TOK, TOK), TOK)
        keyst[:HEAD, at] = moved[:, HEAD:].astype(BF)
        source = block - distance
        wanted = (
            (source >= 0) & (index < SOURCES - 1) & (doc_ref[jnp.maximum(source, 0)] == own_doc)
        )
        bias = jnp.where(wanted, 0.0, NEG)
        keyst[128:144, at] = jnp.where(tile_row == 0, bias, 0.0).astype(BF)
        vext[at, :] = jnp.concatenate([vbuf[32 + inner - distance], ones], axis=1)

    def odd_arrived(distance):
        slot = 32 + inner - distance
        values.arrived(slot)
        maps.arrived(slot)

    def first_keys(step, carry):
        odd_arrived(2 * step + 1)
        carry_keys(2 * step)
        carry_keys(2 * step + 1)
        return carry

    lax.fori_loop(0, CHUNK // 2, first_keys, 0)

    def produce(step, scores, highest):
        chunk = jnp.minimum(step // PAIRS, SOURCES // CHUNK - 1)
        at = pl.ds(pl.multiple_of(chunk * (CHUNK * TOK), TOK), CHUNK * TOK)
        made = nn(qext[step % PAIRS], keyst[:, at])
        scores[...] = made
        highest[...] = jnp.broadcast_to(jnp.max(made, axis=1, keepdims=True), highest.shape)

    def consume(step, scores, highest):
        g = step % PAIRS
        at = pl.ds(pl.multiple_of(step // PAIRS * (CHUNK * TOK), TOK), CHUNK * TOK)
        old = peaks[g]
        peak = jnp.maximum(old, highest[...])
        factor = jnp.exp2(old - peak)
        spread = jnp.concatenate([peak] * (CHUNK * TOK // HEAD), axis=1)
        weights = jnp.exp2(scores[...] - spread).astype(BF)
        accs[g] = accs[g] * jnp.concatenate([factor, factor], axis=1) + nn(weights, vext[at, :])
        peaks[g] = peak

    produce(0, score_a, high_a)

    def absorb(i, carry):
        pl.when(i + AHEAD + 3 <= 16)(lambda: forward(i + AHEAD + 3))
        pl.when(i < 14)(lambda: odd_arrived(2 * i + 5))
        produce(2 * i + 1, score_b, high_b)
        carry_keys(2 * i + 4)
        carry_keys(2 * i + 5)
        consume(2 * i, score_a, high_a)
        produce(2 * i + 2, score_a, high_a)
        consume(2 * i + 1, score_b, high_b)
        return carry

    lax.fori_loop(0, SOURCES // CHUNK * PAIRS // 2, absorb, 0)

    def finish(g, carry):
        for half_pair in range(2):
            total = accs[g, half_pair * TOK : half_pair * TOK + TOK, :]
            at = pl.ds(pl.multiple_of((g * 2 + half_pair) * HEAD, HEAD), HEAD)
            out_ref[:, at] = (total[:, :HEAD] / total[:, HEAD:]).astype(BF)
        return carry

    lax.fori_loop(0, PAIRS, finish, 0)
    values.drain()
    maps.drain()
    for mover in (values, maps):
        for e in range(17):
            when = {0: core == 0, 16: core == 1}.get(e)
            guarded(when, mover.across(32 + inner - 2 * e, e).wait_send)


def local(queries, keys, values, reflect, reflect_logit, doc_of_block):
    vmem = pl.BlockSpec(memory_space=pltpu.VMEM)
    return pl.pallas_call(
        kernel,
        out_shape=jax.ShapeDtypeStruct(queries.shape, BF),
        in_specs=[vmem] * 5 + [pl.BlockSpec(memory_space=pltpu.SMEM)],
        out_specs=vmem,
        scratch_shapes=[
            pltpu.VMEM((SLOTS, TOK, HEAD), BF),
            pltpu.VMEM((SLOTS, HEAD, HEAD + TOK), BF),
            pltpu.VMEM((PAIRS, 2 * TOK, 2 * HEAD), BF),
            pltpu.VMEM((2 * HEAD, (SOURCES + CHUNK) * TOK), BF),
            pltpu.VMEM(((SOURCES + CHUNK) * TOK, 2 * HEAD), BF),
            pltpu.VMEM((PAIRS, 2 * TOK, 2 * HEAD), F32),
            pltpu.VMEM((PAIRS, 2 * TOK, HEAD), F32),
            pltpu.VMEM((HEAD, HEAD), F32),
            pltpu.VMEM((2 * TOK, CHUNK * TOK), F32),
            pltpu.VMEM((2 * TOK, CHUNK * TOK), F32),
            pltpu.VMEM((2 * TOK, HEAD), F32),
            pltpu.VMEM((2 * TOK, HEAD), F32),
            pltpu.SemaphoreType.DMA((SLOTS,)),
            pltpu.SemaphoreType.DMA((SLOTS,)),
            pltpu.SemaphoreType.DMA((SENDS + 17,)),
            pltpu.SemaphoreType.DMA((SENDS + 17,)),
            pltpu.SemaphoreType.DMA,
        ],
        compiler_params=pltpu.CompilerParams(
            collective_id=0, has_side_effects=True, vmem_limit_bytes=48 * 1024 * 1024
        ),
    )(queries, keys, values, reflect, reflect_logit.reshape(1, TOK), doc_of_block)


def solution(mesh):
    placed = (
        P(("outer", "inner"), None),
        P(("outer", "inner"), None),
        P(("outer", "inner"), None),
        P(("outer", "inner"), None),
        P(("outer", "inner")),
        P(),
    )
    return jax.shard_map(
        local, mesh=mesh, in_specs=placed, out_specs=P(("outer", "inner"), None), check_vma=False
    )
```

```python
import functools
import math

import jax
import jax.numpy as jnp
from jax import lax
from jax.experimental import pallas as pl
from jax.experimental.pallas import tpu as pltpu
from jax.sharding import PartitionSpec as P

F32 = jnp.float32
BF = jnp.bfloat16
MESH = pl.DeviceIdType.MESH
NEG = -1e30
TOK = 256
HEAD = 128
HEADS = 8
INNER = 16
SLOTS = 48
CHUNK = 4
SOURCES = 32
PAIRS = 4
TAGS = [("x", 1, 0), ("x", 2, 0)] + [(k, age, 0) for age in range(3) for k in "zy"] + [("y", age, 1) for age in range(3)]
SENDS = 23
AHEAD = 1
SCALE = math.log2(math.e) / math.sqrt(HEAD)


def nn(a, b):
    return jnp.dot(a, b, preferred_element_type=F32)


def nt(a, b):
    return lax.dot_general(a, b, (((1,), (1,)), ((), ())), preferred_element_type=F32)


def split(x):
    hi = x.astype(BF)
    return hi, (x - hi.astype(F32)).astype(BF)


def mm3(a, b):
    ah, al = split(a)
    bh, bl = split(b)
    return nn(ah, bh) + (nn(ah, bl) + nn(al, bh))


def inverse_pair(first, second):
    half = first.shape[0]
    eye = (
        lax.broadcasted_iota(jnp.int32, (half, half), 0)
        == lax.broadcasted_iota(jnp.int32, (half, half), 1)
    ).astype(F32)
    powers = [-first, -second]
    results = [eye + p for p in powers]
    powers = [mm3(p, p) for p in powers]
    reach = 4
    while reach < half:
        stacked = [jnp.concatenate([r, p], axis=0) for r, p in zip(results, powers)]
        grown = [mm3(s, p) for s, p in zip(stacked, powers)]
        results = [r + g[:half] for r, g in zip(results, grown)]
        powers = [g[half:] for g in grown]
        reach *= 2
    return [r + mm3(r, p) for r, p in zip(results, powers)]


def kernel(
    q_hbm, k_hbm, v_hbm, w_hbm, logit_hbm, doc_hbm, out_ref,
    q_ref, k_ref, w_ref, logit_ref, doc_ref,
    vbuf, tkbuf, qext, keyst, vext, accs, peaks, chain, score_a, score_b, high_a, high_b,
    v_recv, tk_recv, v_send, tk_send, local_sems,
):
    outer = lax.axis_index("outer")
    inner = lax.axis_index("inner")
    groups = lax.axis_size("outer")
    block = outer * INNER + inner
    y = inner // 4
    zl = (inner // 2) % 2
    core = inner % 2

    def at_inner(ny, nz, nc):
        return ny * 4 + nz * 2 + nc

    z_peer = (outer, at_inner(y, 1 - zl, core))
    core_peer = (outer, at_inner(y, zl, 1 - core))
    y_peers = [(outer, at_inner((y + dy) % 4, zl, core)) for dy in (1, 2, 3)]
    partner = at_inner(y, 1 - zl, core)
    x_peers = [((outer + d) % groups, inner) for d in (1, 2)]
    x_back = [((outer + groups - d) % groups, inner) for d in (1, 2)]

    loads = [
        pltpu.make_async_copy(source, target, local_sems.at[n])
        for n, (source, target) in enumerate(
            [
                (v_hbm, vbuf.at[32 + inner]),
                (w_hbm, w_ref),
                (k_hbm, k_ref),
                (logit_hbm, logit_ref),
                (doc_hbm, doc_ref),
                (q_hbm, q_ref),
            ]
        )
    ]
    for load in loads:
        load.start()

    barrier = pltpu.get_barrier_semaphore()
    near = [z_peer, core_peer] + y_peers

    def greet(peer):
        pl.semaphore_signal(barrier, inc=1, device_id=peer, device_id_type=MESH)

    for peer in near:
        greet(peer)
    for age, peer in zip((1, 2), x_back):
        pl.when(outer >= age)(functools.partial(greet, peer))
    for load in loads:
        load.wait()

    def guarded(when, action):
        if when is None:
            action()
        else:
            pl.when(when)(action)

    class Mover:
        def __init__(self, buf, send, recv):
            self.buf, self.send, self.recv = buf, send, recv

        def copies(self, tag):
            kind, age, side = tag
            if kind == "x":
                moves = [(32 + inner, 32 - 16 * age + inner, x_peers[age - 1], outer + age < groups)]
            else:
                source = inner if side == 0 else partner
                slot = 32 - 16 * age + source
                if kind == "z":
                    moves = [(slot, slot, z_peer, None)]
                else:
                    moves = [
                        (slot, slot, peer, (y + dy < 4, None, y + dy >= 4)[age])
                        for dy, peer in zip((1, 2, 3), y_peers)
                    ]
            first = sum(3 if t[0] == "y" else 1 for t in TAGS[: TAGS.index(tag)])
            for number, (start, target, peer, when) in enumerate(moves):
                made = pltpu.make_async_remote_copy(
                    src_ref=self.buf.at[start],
                    dst_ref=self.buf.at[target],
                    send_sem=self.send.at[first + number],
                    recv_sem=self.recv.at[target],
                    device_id=peer,
                    device_id_type=MESH,
                )
                yield when, made

        def begin_copies(self, *tag):
            for when, made in self.copies(tag):
                guarded(when, made.start)

        def across(self, slot, number):
            return pltpu.make_async_remote_copy(
                src_ref=self.buf.at[slot],
                dst_ref=self.buf.at[slot],
                send_sem=self.send.at[SENDS + number],
                recv_sem=self.recv.at[slot],
                device_id=core_peer,
                device_id_type=MESH,
            )

        def arrived(self, slot):
            self.across(slot, 0).wait_recv()

        def drain(self):
            for tag in TAGS:
                for when, made in self.copies(tag):
                    guarded(when, made.wait_send)

        def begin(self):
            self.begin_copies("z", 0, 0)
            guarded(core == 0, self.across(32 + inner, 0).start)
            self.begin_copies("y", 0, 0)

        def x_begin(self, age):
            self.begin_copies("x", age, 0)
            slot = 32 - 16 * age + inner
            pl.when(outer < age)(
                lambda: pltpu.make_async_copy(
                    self.buf.at[32 + inner], self.buf.at[slot], self.recv.at[slot]
                ).start()
            )

        def after_z(self, age):
            self.arrived(32 - 16 * age + partner)
            self.begin_copies("y", age, 1)

        def after_x(self, age):
            self.arrived(32 - 16 * age + inner)
            self.begin_copies("z", age, 0)
            self.begin_copies("y", age, 0)

    values = Mover(vbuf, v_send, v_recv)
    maps = Mover(tkbuf, tk_send, tk_recv)


    w0 = w_ref[...]
    key_rows = k_ref[...]
    rows = lax.broadcasted_iota(jnp.int32, (TOK, TOK), 0)
    cols = lax.broadcasted_iota(jnp.int32, (TOK, TOK), 1)
    eye = rows == cols
    gram = nt(w0, w0)
    diagonal = jnp.where(eye, gram, 0.0)
    norm_col = lax.rsqrt(jnp.sum(diagonal, axis=1, keepdims=True) + 1e-6)
    norm_row = lax.rsqrt(jnp.sum(diagonal, axis=0, keepdims=True) + 1e-6)
    beta_row = 2.0 / (1.0 + jnp.exp(-logit_ref[...]))
    beta_col = jnp.sum(
        jnp.where(eye, jnp.broadcast_to(beta_row, (TOK, TOK)), 0.0), axis=1, keepdims=True
    )
    reach_row = norm_row * beta_row
    below = rows > cols
    strict = jnp.where(below, gram * norm_col * reach_row, 0.0)
    cross = jnp.where(below, nt(w0, key_rows) * norm_col, 0.0)
    unit = w0.astype(F32) * norm_col
    right = jnp.concatenate([unit, cross], axis=1)
    half = TOK // 2
    pl.semaphore_wait(barrier, len(near) + jnp.minimum(groups - 1 - outer, 2))
    values.x_begin(1)
    values.begin()
    inv_first, inv_second = inverse_pair(strict[:half, :half], strict[half:, half:])
    solved_first = mm3(inv_first, right[:half])
    solved_second = mm3(inv_second, right[half:] - mm3(strict[half:, :half], solved_first))
    solved = jnp.concatenate([solved_first, solved_second], axis=0)
    scaled_t = (unit * beta_col).T
    key_t = key_rows.astype(F32).T
    eye_head = (
        lax.broadcasted_iota(jnp.int32, (HEAD, HEAD), 0)
        == lax.broadcasted_iota(jnp.int32, (HEAD, HEAD), 1)
    ).astype(F32)
    own_map = jnp.concatenate([eye_head, key_t], axis=1) - mm3(scaled_t, solved)
    tkbuf[32 + inner] = own_map.astype(BF)
    solved_hi = solved.astype(BF)

    maps.x_begin(1)
    maps.begin()
    values.x_begin(2)
    maps.x_begin(2)

    ones = jnp.ones((TOK, HEAD), BF)
    visible = rows >= cols
    lanes = lax.broadcasted_iota(jnp.int32, (TOK, HEAD), 1)
    first_lane = jnp.where(lanes == 0, 1.0, 0.0).astype(BF)

    own_values = jnp.concatenate([vbuf[32 + inner], ones], axis=1)

    def prepare_head(h, g, at):
        q = q_ref[:, pl.ds(pl.multiple_of(h * HEAD, HEAD), HEAD)]
        facing = jnp.where(visible, nt(q, w0) * reach_row, 0.0)
        face_hi = facing.astype(BF)
        moved = nn(face_hi, solved_hi)
        turned = (q.astype(F32) - moved[:, :HEAD]) * SCALE
        qext[g, at, :] = jnp.concatenate([turned.astype(BF), first_lane], axis=1)
        inside = (nt(q, key_rows) - moved[:, HEAD:]) * SCALE
        inside = jnp.where(visible, inside, NEG)
        peak = jnp.max(inside, axis=1, keepdims=True)
        weights = jnp.exp2(inside - peak).astype(BF)
        accs[g, at, :] = nn(weights, own_values)
        peaks[g, at, :] = jnp.broadcast_to(peak, (TOK, HEAD))

    def prepare_pair(g, carry):
        for half_pair in range(2):
            prepare_head(g * 2 + half_pair, g, slice(half_pair * TOK, half_pair * TOK + TOK))
        pl.when(g == 0)(lambda: values.after_z(0))
        pl.when(g == 1)(lambda: maps.after_z(0))
        pl.when(g == 2)(lambda: values.after_x(1))
        return carry

    lax.fori_loop(0, PAIRS, prepare_pair, 0)
    maps.after_x(1)
    values.after_z(1)
    maps.after_z(1)

    def forward(e):
        slot = 32 + inner - 2 * e

        @pl.when((slot % INNER // 4 != y) & (e < 16))
        def _():
            values.arrived(slot)
            maps.arrived(slot)

        @pl.when((e < 16) | (core == 1))
        def _():
            values.across(slot, e).start()
            maps.across(slot, e).start()

    def forward_step(e, carry):
        forward(e)
        return carry

    lax.fori_loop(1, AHEAD + 3, forward_step, 0)

    keyst[128:, :] = jnp.zeros((128, keyst.shape[1]), BF)
    tile_row = lax.broadcasted_iota(jnp.int32, (16, TOK), 0)
    chain[...] = eye_head
    own_doc = doc_ref[block]

    def carry_keys(index):
        distance = jnp.minimum(index + 1, SOURCES - 1)
        hi, lo = split(chain[...])
        both = tkbuf[32 + inner - distance]
        moved = nn(hi, both)
        chain[...] = moved[:, :HEAD] + nn(lo, both[:, :HEAD])
        at = pl.ds(pl.multiple_of(index * TOK, TOK), TOK)
        keyst[:HEAD, at] = moved[:, HEAD:].astype(BF)
        source = block - distance
        wanted = (
            (source >= 0) & (index < SOURCES - 1) & (doc_ref[jnp.maximum(source, 0)] == own_doc)
        )
        bias = jnp.where(wanted, 0.0, NEG)
        keyst[128:144, at] = jnp.where(tile_row == 0, bias, 0.0).astype(BF)
        vext[at, :] = jnp.concatenate([vbuf[32 + inner - distance], ones], axis=1)

    def odd_arrived(distance):
        slot = 32 + inner - distance
        values.arrived(slot)
        maps.arrived(slot)

    def first_keys(step, carry):
        odd_arrived(2 * step + 1)
        carry_keys(2 * step)
        carry_keys(2 * step + 1)
        return carry

    lax.fori_loop(0, CHUNK // 2, first_keys, 0)

    def produce(step, scores, highest):
        chunk = jnp.minimum(step // PAIRS, SOURCES // CHUNK - 1)
        at = pl.ds(pl.multiple_of(chunk * (CHUNK * TOK), TOK), CHUNK * TOK)
        made = nn(qext[step % PAIRS], keyst[:, at])
        scores[...] = made
        highest[...] = jnp.broadcast_to(jnp.max(made, axis=1, keepdims=True), highest.shape)

    def consume(step, scores, highest):
        g = step % PAIRS
        at = pl.ds(pl.multiple_of(step // PAIRS * (CHUNK * TOK), TOK), CHUNK * TOK)
        old = peaks[g]
        peak = jnp.maximum(old, highest[...])
        factor = jnp.exp2(old - peak)
        spread = jnp.concatenate([peak] * (CHUNK * TOK // HEAD), axis=1)
        weights = jnp.exp2(scores[...] - spread).astype(BF)
        accs[g] = accs[g] * jnp.concatenate([factor, factor], axis=1) + nn(weights, vext[at, :])
        peaks[g] = peak

    produce(0, score_a, high_a)

    def absorb(i, carry):
        pl.when(i == 1)(lambda: values.after_x(2))

        @pl.when(i == 3)
        def _():
            maps.after_x(2)
            values.after_z(2)

        pl.when(i == 5)(lambda: maps.after_z(2))
        pl.when(i + AHEAD + 3 <= 16)(lambda: forward(i + AHEAD + 3))
        pl.when(i < 14)(lambda: odd_arrived(2 * i + 5))
        produce(2 * i + 1, score_b, high_b)
        carry_keys(2 * i + 4)
        carry_keys(2 * i + 5)
        consume(2 * i, score_a, high_a)
        produce(2 * i + 2, score_a, high_a)
        consume(2 * i + 1, score_b, high_b)
        return carry

    lax.fori_loop(0, SOURCES // CHUNK * PAIRS // 2, absorb, 0)

    def finish(g, carry):
        for half_pair in range(2):
            total = accs[g, half_pair * TOK : half_pair * TOK + TOK, :]
            at = pl.ds(pl.multiple_of((g * 2 + half_pair) * HEAD, HEAD), HEAD)
            out_ref[:, at] = (total[:, :HEAD] / total[:, HEAD:]).astype(BF)
        return carry

    lax.fori_loop(0, PAIRS, finish, 0)
    values.drain()
    maps.drain()
    for mover in (values, maps):
        for e in range(17):
            when = {0: core == 0, 16: core == 1}.get(e)
            guarded(when, mover.across(32 + inner - 2 * e, e).wait_send)


def local(queries, keys, values, reflect, reflect_logit, doc_of_block):
    vmem = pl.BlockSpec(memory_space=pltpu.VMEM)
    return pl.pallas_call(
        kernel,
        out_shape=jax.ShapeDtypeStruct(queries.shape, BF),
        in_specs=[pl.BlockSpec(memory_space=pltpu.HBM)] * 6,
        out_specs=vmem,
        scratch_shapes=[
            pltpu.VMEM((TOK, HEADS * HEAD), BF),
            pltpu.VMEM((TOK, HEAD), BF),
            pltpu.VMEM((TOK, HEAD), BF),
            pltpu.VMEM((1, TOK), F32),
            pltpu.SMEM((256,), jnp.int32),
            pltpu.VMEM((SLOTS, TOK, HEAD), BF),
            pltpu.VMEM((SLOTS, HEAD, HEAD + TOK), BF),
            pltpu.VMEM((PAIRS, 2 * TOK, 2 * HEAD), BF),
            pltpu.VMEM((2 * HEAD, (SOURCES + CHUNK) * TOK), BF),
            pltpu.VMEM(((SOURCES + CHUNK) * TOK, 2 * HEAD), BF),
            pltpu.VMEM((PAIRS, 2 * TOK, 2 * HEAD), F32),
            pltpu.VMEM((PAIRS, 2 * TOK, HEAD), F32),
            pltpu.VMEM((HEAD, HEAD), F32),
            pltpu.VMEM((2 * TOK, CHUNK * TOK), F32),
            pltpu.VMEM((2 * TOK, CHUNK * TOK), F32),
            pltpu.VMEM((2 * TOK, HEAD), F32),
            pltpu.VMEM((2 * TOK, HEAD), F32),
            pltpu.SemaphoreType.DMA((SLOTS,)),
            pltpu.SemaphoreType.DMA((SLOTS,)),
            pltpu.SemaphoreType.DMA((SENDS + 17,)),
            pltpu.SemaphoreType.DMA((SENDS + 17,)),
            pltpu.SemaphoreType.DMA((6,)),
        ],
        compiler_params=pltpu.CompilerParams(
            collective_id=0, has_side_effects=True, vmem_limit_bytes=63 * 1024 * 1024
        ),
    )(queries, keys, values, reflect, reflect_logit.reshape(1, TOK), doc_of_block)


def solution(mesh):
    placed = (
        P(("outer", "inner"), None),
        P(("outer", "inner"), None),
        P(("outer", "inner"), None),
        P(("outer", "inner"), None),
        P(("outer", "inner")),
        P(),
    )
    return jax.shard_map(
        local, mesh=mesh, in_specs=placed, out_specs=P(("outer", "inner"), None), check_vma=False
    )
```

```python
import functools
import math

import jax
import jax.numpy as jnp
from jax import lax
from jax.experimental import pallas as pl
from jax.experimental.pallas import tpu as pltpu
from jax.sharding import PartitionSpec as P

F32 = jnp.float32
BF = jnp.bfloat16
MESH = pl.DeviceIdType.MESH
NEG = -1e30
TOK = 256
HEAD = 128
HEADS = 8
INNER = 16
SLOTS = 48
CHUNK = 4
SOURCES = 32
PAIRS = 4
TAGS = [(kind, age, 0) for kind in "xp" for age in (1, 2)] + [(k, age, 0) for age in range(3) for k in "zy"] + [("y", age, 1) for age in range(3)]
SENDS = 25
AHEAD = 1
SCALE = math.log2(math.e) / math.sqrt(HEAD)


def nn(a, b):
    return jnp.dot(a, b, preferred_element_type=F32)


def nt(a, b):
    return lax.dot_general(a, b, (((1,), (1,)), ((), ())), preferred_element_type=F32)


def split(x):
    hi = x.astype(BF)
    return hi, (x - hi.astype(F32)).astype(BF)


def mm3(a, b):
    ah, al = split(a)
    bh, bl = split(b)
    return nn(ah, bh) + (nn(ah, bl) + nn(al, bh))


def inverse_pair(first, second):
    half = first.shape[0]
    eye = (
        lax.broadcasted_iota(jnp.int32, (half, half), 0)
        == lax.broadcasted_iota(jnp.int32, (half, half), 1)
    ).astype(F32)
    powers = [-first, -second]
    results = [eye + p for p in powers]
    powers = [mm3(p, p) for p in powers]
    reach = 4
    while reach < half:
        stacked = [jnp.concatenate([r, p], axis=0) for r, p in zip(results, powers)]
        grown = [mm3(s, p) for s, p in zip(stacked, powers)]
        results = [r + g[:half] for r, g in zip(results, grown)]
        powers = [g[half:] for g in grown]
        reach *= 2
    return [r + mm3(r, p) for r, p in zip(results, powers)]


def kernel(
    q_hbm, k_hbm, v_hbm, w_hbm, logit_hbm, doc_hbm, out_ref,
    q_ref, k_ref, w_ref, logit_ref, doc_ref,
    vbuf, tkbuf, qext, keyst, vext, accs, peaks, chain, score_a, score_b, high_a, high_b,
    v_recv, tk_recv, v_send, tk_send, local_sems,
):
    outer = lax.axis_index("outer")
    inner = lax.axis_index("inner")
    groups = lax.axis_size("outer")
    block = outer * INNER + inner
    y = inner // 4
    zl = (inner // 2) % 2
    core = inner % 2

    def at_inner(ny, nz, nc):
        return ny * 4 + nz * 2 + nc

    partner = at_inner(y, 1 - zl, core)
    z_peer = (outer, at_inner(y, 1 - zl, core))
    core_peer = (outer, at_inner(y, zl, 1 - core))
    y_peers = [(outer, at_inner((y + dy) % 4, zl, core)) for dy in (1, 2, 3)]
    x_peer = ((outer + 1) % groups, inner)
    x_partner = ((outer + 1) % groups, partner)
    turning = outer % 4 == 3
    more = outer + 1 < groups
    sends_own = more & jnp.logical_not(turning & (zl == 0))
    sends_both = more & turning & (zl == 1)
    from_partner = (outer % 4 == 0) & (zl == 0)
    x_back = ((outer + groups - 1) % groups, jnp.where(from_partner, partner, inner))
    expected = jnp.where(more, jnp.where(turning, 2 * zl, 1), 0)

    loads = [
        pltpu.make_async_copy(source, target, local_sems.at[n])
        for n, (source, target) in enumerate(
            [
                (v_hbm, vbuf.at[32 + inner]),
                (w_hbm, w_ref),
                (k_hbm, k_ref),
                (logit_hbm, logit_ref),
                (doc_hbm, doc_ref),
                (q_hbm, q_ref),
            ]
        )
    ]
    for load in loads:
        load.start()

    barrier = pltpu.get_barrier_semaphore()
    near = [z_peer, core_peer] + y_peers

    def greet(peer):
        pl.semaphore_signal(barrier, inc=1, device_id=peer, device_id_type=MESH)

    for peer in near:
        greet(peer)
    pl.when(outer >= 1)(functools.partial(greet, x_back))
    for load in loads:
        load.wait()

    def guarded(when, action):
        if when is None:
            action()
        else:
            pl.when(when)(action)

    class Mover:
        def __init__(self, buf, send, recv):
            self.buf, self.send, self.recv = buf, send, recv

        def copies(self, tag):
            kind, age, side = tag
            if kind == "x":
                moves = [(48 - 16 * age + inner, 32 - 16 * age + inner, x_peer, sends_own)]
            elif kind == "p":
                moves = [(48 - 16 * age + partner, 32 - 16 * age + partner, x_partner, sends_both)]
            else:
                source = inner if side == 0 else partner
                slot = 32 - 16 * age + source
                if kind == "z":
                    moves = [(slot, slot, z_peer, None)]
                else:
                    moves = [
                        (slot, slot, peer, (y + dy < 4, None, y + dy >= 4)[age])
                        for dy, peer in zip((1, 2, 3), y_peers)
                    ]
            first = sum(3 if t[0] == "y" else 1 for t in TAGS[: TAGS.index(tag)])
            for number, (start, target, peer, when) in enumerate(moves):
                made = pltpu.make_async_remote_copy(
                    src_ref=self.buf.at[start],
                    dst_ref=self.buf.at[target],
                    send_sem=self.send.at[first + number],
                    recv_sem=self.recv.at[target],
                    device_id=peer,
                    device_id_type=MESH,
                )
                yield when, made

        def begin_copies(self, *tag):
            for when, made in self.copies(tag):
                guarded(when, made.start)

        def across(self, slot, number):
            return pltpu.make_async_remote_copy(
                src_ref=self.buf.at[slot],
                dst_ref=self.buf.at[slot],
                send_sem=self.send.at[SENDS + number],
                recv_sem=self.recv.at[slot],
                device_id=core_peer,
                device_id_type=MESH,
            )

        def arrived(self, slot):
            self.across(slot, 0).wait_recv()

        def drain(self):
            for tag in TAGS:
                for when, made in self.copies(tag):
                    guarded(when, made.wait_send)

        def begin(self):
            self.begin_copies("z", 0, 0)
            guarded(core == 0, self.across(32 + inner, 0).start)
            self.begin_copies("y", 0, 0)

        def x_begin(self, age):
            self.begin_copies("x", age, 0)
            slot = 32 - 16 * age + inner
            pl.when(outer == 0)(
                lambda: pltpu.make_async_copy(
                    self.buf.at[32 + inner], self.buf.at[slot], self.recv.at[slot]
                ).start()
            )

        def after_z(self, age):
            self.arrived(32 - 16 * age + partner)
            if age < 2:
                self.begin_copies("p", age + 1, 0)
            self.begin_copies("y", age, 1)

        def after_x(self, age):
            self.arrived(32 - 16 * age + inner)
            self.begin_copies("z", age, 0)
            if age < 2:
                self.x_begin(age + 1)
            self.begin_copies("y", age, 0)

    values = Mover(vbuf, v_send, v_recv)
    maps = Mover(tkbuf, tk_send, tk_recv)


    w0 = w_ref[...]
    key_rows = k_ref[...]
    rows = lax.broadcasted_iota(jnp.int32, (TOK, TOK), 0)
    cols = lax.broadcasted_iota(jnp.int32, (TOK, TOK), 1)
    eye = rows == cols
    gram = nt(w0, w0)
    diagonal = jnp.where(eye, gram, 0.0)
    norm_col = lax.rsqrt(jnp.sum(diagonal, axis=1, keepdims=True) + 1e-6)
    norm_row = lax.rsqrt(jnp.sum(diagonal, axis=0, keepdims=True) + 1e-6)
    beta_row = 2.0 / (1.0 + jnp.exp(-logit_ref[...]))
    beta_col = jnp.sum(
        jnp.where(eye, jnp.broadcast_to(beta_row, (TOK, TOK)), 0.0), axis=1, keepdims=True
    )
    reach_row = norm_row * beta_row
    below = rows > cols
    strict = jnp.where(below, gram * norm_col * reach_row, 0.0)
    cross = jnp.where(below, nt(w0, key_rows) * norm_col, 0.0)
    unit = w0.astype(F32) * norm_col
    right = jnp.concatenate([unit, cross], axis=1)
    half = TOK // 2
    pl.semaphore_wait(barrier, len(near) + expected)
    values.x_begin(1)
    values.begin()
    inv_first, inv_second = inverse_pair(strict[:half, :half], strict[half:, half:])
    solved_first = mm3(inv_first, right[:half])
    solved_second = mm3(inv_second, right[half:] - mm3(strict[half:, :half], solved_first))
    solved = jnp.concatenate([solved_first, solved_second], axis=0)
    scaled_t = (unit * beta_col).T
    key_t = key_rows.astype(F32).T
    eye_head = (
        lax.broadcasted_iota(jnp.int32, (HEAD, HEAD), 0)
        == lax.broadcasted_iota(jnp.int32, (HEAD, HEAD), 1)
    ).astype(F32)
    own_map = jnp.concatenate([eye_head, key_t], axis=1) - mm3(scaled_t, solved)
    tkbuf[32 + inner] = own_map.astype(BF)
    solved_hi = solved.astype(BF)

    maps.x_begin(1)
    maps.begin()

    ones = jnp.ones((TOK, HEAD), BF)
    visible = rows >= cols
    lanes = lax.broadcasted_iota(jnp.int32, (TOK, HEAD), 1)
    first_lane = jnp.where(lanes == 0, 1.0, 0.0).astype(BF)

    own_values = jnp.concatenate([vbuf[32 + inner], ones], axis=1)

    def prepare_head(h, g, at):
        q = q_ref[:, pl.ds(pl.multiple_of(h * HEAD, HEAD), HEAD)]
        facing = jnp.where(visible, nt(q, w0) * reach_row, 0.0)
        face_hi = facing.astype(BF)
        moved = nn(face_hi, solved_hi)
        turned = (q.astype(F32) - moved[:, :HEAD]) * SCALE
        qext[g, at, :] = jnp.concatenate([turned.astype(BF), first_lane], axis=1)
        inside = (nt(q, key_rows) - moved[:, HEAD:]) * SCALE
        inside = jnp.where(visible, inside, NEG)
        peak = jnp.max(inside, axis=1, keepdims=True)
        weights = jnp.exp2(inside - peak).astype(BF)
        accs[g, at, :] = nn(weights, own_values)
        peaks[g, at, :] = jnp.broadcast_to(peak, (TOK, HEAD))

    def prepare_pair(g, carry):
        for half_pair in range(2):
            prepare_head(g * 2 + half_pair, g, slice(half_pair * TOK, half_pair * TOK + TOK))
        pl.when(g == 0)(lambda: values.after_z(0))
        pl.when(g == 1)(lambda: values.after_x(1))
        pl.when(g == 2)(lambda: maps.after_z(0))
        return carry

    lax.fori_loop(0, PAIRS, prepare_pair, 0)
    values.after_z(1)
    maps.after_x(1)
    maps.after_z(1)

    def forward(e):
        slot = 32 + inner - 2 * e

        @pl.when((slot % INNER // 4 != y) & (e < 16))
        def _():
            values.arrived(slot)
            maps.arrived(slot)

        @pl.when((e < 16) | (core == 1))
        def _():
            values.across(slot, e).start()
            maps.across(slot, e).start()

    def forward_step(e, carry):
        forward(e)
        return carry

    lax.fori_loop(1, AHEAD + 3, forward_step, 0)

    keyst[128:, :] = jnp.zeros((128, keyst.shape[1]), BF)
    tile_row = lax.broadcasted_iota(jnp.int32, (16, TOK), 0)
    chain[...] = eye_head
    own_doc = doc_ref[block]

    def carry_keys(index):
        distance = jnp.minimum(index + 1, SOURCES - 1)
        hi, lo = split(chain[...])
        both = tkbuf[32 + inner - distance]
        moved = nn(hi, both)
        chain[...] = moved[:, :HEAD] + nn(lo, both[:, :HEAD])
        at = pl.ds(pl.multiple_of(index * TOK, TOK), TOK)
        keyst[:HEAD, at] = moved[:, HEAD:].astype(BF)
        source = block - distance
        wanted = (
            (source >= 0) & (index < SOURCES - 1) & (doc_ref[jnp.maximum(source, 0)] == own_doc)
        )
        bias = jnp.where(wanted, 0.0, NEG)
        keyst[128:144, at] = jnp.where(tile_row == 0, bias, 0.0).astype(BF)
        vext[at, :] = jnp.concatenate([vbuf[32 + inner - distance], ones], axis=1)

    def odd_arrived(distance):
        slot = 32 + inner - distance
        values.arrived(slot)
        maps.arrived(slot)

    def first_keys(step, carry):
        odd_arrived(2 * step + 1)
        carry_keys(2 * step)
        carry_keys(2 * step + 1)
        return carry

    lax.fori_loop(0, CHUNK // 2, first_keys, 0)

    def produce(step, scores, highest):
        chunk = jnp.minimum(step // PAIRS, SOURCES // CHUNK - 1)
        at = pl.ds(pl.multiple_of(chunk * (CHUNK * TOK), TOK), CHUNK * TOK)
        made = nn(qext[step % PAIRS], keyst[:, at])
        scores[...] = made
        highest[...] = jnp.broadcast_to(jnp.max(made, axis=1, keepdims=True), highest.shape)

    def consume(step, scores, highest):
        g = step % PAIRS
        at = pl.ds(pl.multiple_of(step // PAIRS * (CHUNK * TOK), TOK), CHUNK * TOK)
        old = peaks[g]
        peak = jnp.maximum(old, highest[...])
        factor = jnp.exp2(old - peak)
        spread = jnp.concatenate([peak] * (CHUNK * TOK // HEAD), axis=1)
        weights = jnp.exp2(scores[...] - spread).astype(BF)
        accs[g] = accs[g] * jnp.concatenate([factor, factor], axis=1) + nn(weights, vext[at, :])
        peaks[g] = peak

    produce(0, score_a, high_a)

    def absorb(i, carry):
        pl.when(i == 0)(lambda: values.after_x(2))
        pl.when(i == 1)(lambda: values.after_z(2))
        pl.when(i == 1)(lambda: maps.after_x(2))
        pl.when(i == 3)(lambda: maps.after_z(2))
        pl.when(i + AHEAD + 3 <= 16)(lambda: forward(i + AHEAD + 3))
        pl.when(i < 14)(lambda: odd_arrived(2 * i + 5))
        produce(2 * i + 1, score_b, high_b)
        consume(2 * i, score_a, high_a)
        carry_keys(2 * i + 4)
        carry_keys(2 * i + 5)
        produce(2 * i + 2, score_a, high_a)
        consume(2 * i + 1, score_b, high_b)
        return carry

    lax.fori_loop(0, SOURCES // CHUNK * PAIRS // 2, absorb, 0)

    def finish(g, carry):
        for half_pair in range(2):
            total = accs[g, half_pair * TOK : half_pair * TOK + TOK, :]
            at = pl.ds(pl.multiple_of((g * 2 + half_pair) * HEAD, HEAD), HEAD)
            out_ref[:, at] = (total[:, :HEAD] / total[:, HEAD:]).astype(BF)
        return carry

    lax.fori_loop(0, PAIRS, finish, 0)
    values.drain()
    maps.drain()
    for mover in (values, maps):
        for e in range(17):
            when = {0: core == 0, 16: core == 1}.get(e)
            guarded(when, mover.across(32 + inner - 2 * e, e).wait_send)


def local(queries, keys, values, reflect, reflect_logit, doc_of_block):
    vmem = pl.BlockSpec(memory_space=pltpu.VMEM)
    return pl.pallas_call(
        kernel,
        out_shape=jax.ShapeDtypeStruct(queries.shape, BF),
        in_specs=[pl.BlockSpec(memory_space=pltpu.HBM)] * 6,
        out_specs=vmem,
        scratch_shapes=[
            pltpu.VMEM((TOK, HEADS * HEAD), BF),
            pltpu.VMEM((TOK, HEAD), BF),
            pltpu.VMEM((TOK, HEAD), BF),
            pltpu.VMEM((1, TOK), F32),
            pltpu.SMEM((256,), jnp.int32),
            pltpu.VMEM((SLOTS, TOK, HEAD), BF),
            pltpu.VMEM((SLOTS, HEAD, HEAD + TOK), BF),
            pltpu.VMEM((PAIRS, 2 * TOK, 2 * HEAD), BF),
            pltpu.VMEM((2 * HEAD, (SOURCES + CHUNK) * TOK), BF),
            pltpu.VMEM(((SOURCES + CHUNK) * TOK, 2 * HEAD), BF),
            pltpu.VMEM((PAIRS, 2 * TOK, 2 * HEAD), F32),
            pltpu.VMEM((PAIRS, 2 * TOK, HEAD), F32),
            pltpu.VMEM((HEAD, HEAD), F32),
            pltpu.VMEM((2 * TOK, CHUNK * TOK), F32),
            pltpu.VMEM((2 * TOK, CHUNK * TOK), F32),
            pltpu.VMEM((2 * TOK, HEAD), F32),
            pltpu.VMEM((2 * TOK, HEAD), F32),
            pltpu.SemaphoreType.DMA((SLOTS,)),
            pltpu.SemaphoreType.DMA((SLOTS,)),
            pltpu.SemaphoreType.DMA((SENDS + 17,)),
            pltpu.SemaphoreType.DMA((SENDS + 17,)),
            pltpu.SemaphoreType.DMA((6,)),
        ],
        compiler_params=pltpu.CompilerParams(
            collective_id=0, has_side_effects=True, vmem_limit_bytes=63 * 1024 * 1024
        ),
    )(queries, keys, values, reflect, reflect_logit.reshape(1, TOK), doc_of_block)


def solution(mesh):
    placed = (
        P(("outer", "inner"), None),
        P(("outer", "inner"), None),
        P(("outer", "inner"), None),
        P(("outer", "inner"), None),
        P(("outer", "inner")),
        P(),
    )
    return jax.shard_map(
        local, mesh=mesh, in_specs=placed, out_specs=P(("outer", "inner"), None), check_vma=False
    )
```

```python
import functools
import math

import jax
import jax.numpy as jnp
from jax import lax
from jax.experimental import pallas as pl
from jax.experimental.pallas import tpu as pltpu
from jax.sharding import PartitionSpec as P

F32 = jnp.float32
BF = jnp.bfloat16
MESH = pl.DeviceIdType.MESH
NEG = -1e30
TOK = 256
HEAD = 128
HEADS = 8
INNER = 16
SLOTS = 48
CHUNK = 4
SOURCES = 32
PAIRS = 4
TAGS = [(kind, age, 0) for kind in "xp" for age in (1, 2)] + [(k, age, 0) for age in range(3) for k in "zy"] + [("y", age, 1) for age in range(3)]
SENDS = 25
AHEAD = 1
SCALE = math.log2(math.e) / math.sqrt(HEAD)


def nn(a, b):
    return jnp.dot(a, b, preferred_element_type=F32)


def nt(a, b):
    return lax.dot_general(a, b, (((1,), (1,)), ((), ())), preferred_element_type=F32)


def split(x):
    hi = x.astype(BF)
    return hi, (x - hi.astype(F32)).astype(BF)


def mm3(a, b):
    ah, al = split(a)
    bh, bl = split(b)
    return nn(ah, bh) + (nn(ah, bl) + nn(al, bh))


def inverse_pair(first, second):
    half = first.shape[0]
    eye = (
        lax.broadcasted_iota(jnp.int32, (half, half), 0)
        == lax.broadcasted_iota(jnp.int32, (half, half), 1)
    ).astype(F32)
    powers = [-first, -second]
    results = [eye + p for p in powers]
    powers = [mm3(p, p) for p in powers]
    reach = 4
    while reach < half:
        stacked = [jnp.concatenate([r, p], axis=0) for r, p in zip(results, powers)]
        grown = [mm3(s, p) for s, p in zip(stacked, powers)]
        results = [r + g[:half] for r, g in zip(results, grown)]
        powers = [g[half:] for g in grown]
        reach *= 2
    return [r + mm3(r, p) for r, p in zip(results, powers)]


def kernel(
    q_hbm, k_hbm, v_hbm, w_hbm, logit_hbm, doc_hbm, out_ref,
    q_ref, k_ref, w_ref, logit_ref, doc_ref,
    vbuf, tkbuf, qext, keyst, vext, accs, peaks, chain, score_a, score_b, high_a, high_b,
    v_recv, tk_recv, v_send, tk_send, local_sems,
):
    outer = lax.axis_index("outer")
    inner = lax.axis_index("inner")
    groups = lax.axis_size("outer")
    block = outer * INNER + inner
    y = inner // 4
    zl = (inner // 2) % 2
    core = inner % 2

    def at_inner(ny, nz, nc):
        return ny * 4 + nz * 2 + nc

    partner = at_inner(y, 1 - zl, core)
    z_peer = (outer, at_inner(y, 1 - zl, core))
    core_peer = (outer, at_inner(y, zl, 1 - core))
    y_peers = [(outer, at_inner((y + dy) % 4, zl, core)) for dy in (1, 2, 3)]
    x_peer = ((outer + 1) % groups, inner)
    x_partner = ((outer + 1) % groups, partner)
    turning = outer % 4 == 3
    more = outer + 1 < groups
    sends_own = more & jnp.logical_not(turning & (zl == 0))
    sends_both = more & turning & (zl == 1)
    from_partner = (outer % 4 == 0) & (zl == 0)
    x_back = ((outer + groups - 1) % groups, jnp.where(from_partner, partner, inner))
    expected = jnp.where(more, jnp.where(turning, 2 * zl, 1), 0)

    loads = [
        pltpu.make_async_copy(source, target, local_sems.at[n])
        for n, (source, target) in enumerate(
            [
                (v_hbm, vbuf.at[32 + inner]),
                (w_hbm, w_ref),
                (k_hbm, k_ref),
                (logit_hbm, logit_ref),
                (doc_hbm, doc_ref),
                (q_hbm, q_ref),
            ]
        )
    ]
    for load in loads:
        load.start()

    barrier = pltpu.get_barrier_semaphore()
    near = [z_peer, core_peer] + y_peers

    def greet(peer):
        pl.semaphore_signal(barrier, inc=1, device_id=peer, device_id_type=MESH)

    for peer in near:
        greet(peer)
    pl.when(outer >= 1)(functools.partial(greet, x_back))
    for load in loads:
        load.wait()

    def guarded(when, action):
        if when is None:
            action()
        else:
            pl.when(when)(action)

    class Mover:
        def __init__(self, buf, send, recv):
            self.buf, self.send, self.recv = buf, send, recv

        def copies(self, tag):
            kind, age, side = tag
            if kind == "x":
                moves = [(48 - 16 * age + inner, 32 - 16 * age + inner, x_peer, sends_own)]
            elif kind == "p":
                moves = [(48 - 16 * age + partner, 32 - 16 * age + partner, x_partner, sends_both)]
            else:
                source = inner if side == 0 else partner
                slot = 32 - 16 * age + source
                if kind == "z":
                    moves = [(slot, slot, z_peer, None)]
                else:
                    moves = [
                        (slot, slot, peer, (y + dy < 4, None, y + dy >= 4)[age])
                        for dy, peer in zip((1, 2, 3), y_peers)
                    ]
            first = sum(3 if t[0] == "y" else 1 for t in TAGS[: TAGS.index(tag)])
            for number, (start, target, peer, when) in enumerate(moves):
                made = pltpu.make_async_remote_copy(
                    src_ref=self.buf.at[start],
                    dst_ref=self.buf.at[target],
                    send_sem=self.send.at[first + number],
                    recv_sem=self.recv.at[target],
                    device_id=peer,
                    device_id_type=MESH,
                )
                yield when, made

        def begin_copies(self, *tag):
            for when, made in self.copies(tag):
                guarded(when, made.start)

        def across(self, slot, number):
            return pltpu.make_async_remote_copy(
                src_ref=self.buf.at[slot],
                dst_ref=self.buf.at[slot],
                send_sem=self.send.at[SENDS + number],
                recv_sem=self.recv.at[slot],
                device_id=core_peer,
                device_id_type=MESH,
            )

        def arrived(self, slot):
            self.across(slot, 0).wait_recv()

        def drain(self):
            for tag in TAGS:
                for when, made in self.copies(tag):
                    guarded(when, made.wait_send)

        def begin(self):
            self.begin_copies("z", 0, 0)
            guarded(core == 0, self.across(32 + inner, 0).start)
            self.begin_copies("y", 0, 0)

        def x_begin(self, age):
            self.begin_copies("x", age, 0)
            slot = 32 - 16 * age + inner
            pl.when(outer == 0)(
                lambda: pltpu.make_async_copy(
                    self.buf.at[32 + inner], self.buf.at[slot], self.recv.at[slot]
                ).start()
            )

        def after_z(self, age):
            self.arrived(32 - 16 * age + partner)
            if age < 2:
                self.begin_copies("p", age + 1, 0)
            self.begin_copies("y", age, 1)

        def after_x(self, age):
            self.arrived(32 - 16 * age + inner)
            self.begin_copies("z", age, 0)
            if age < 2:
                self.x_begin(age + 1)
            self.begin_copies("y", age, 0)

    values = Mover(vbuf, v_send, v_recv)
    maps = Mover(tkbuf, tk_send, tk_recv)


    w0 = w_ref[...]
    key_rows = k_ref[...]
    rows = lax.broadcasted_iota(jnp.int32, (TOK, TOK), 0)
    cols = lax.broadcasted_iota(jnp.int32, (TOK, TOK), 1)
    eye = rows == cols
    gram = nt(w0, w0)
    diagonal = jnp.where(eye, gram, 0.0)
    norm_col = lax.rsqrt(jnp.sum(diagonal, axis=1, keepdims=True) + 1e-6)
    norm_row = lax.rsqrt(jnp.sum(diagonal, axis=0, keepdims=True) + 1e-6)
    beta_row = 2.0 / (1.0 + jnp.exp(-logit_ref[...]))
    beta_col = jnp.sum(
        jnp.where(eye, jnp.broadcast_to(beta_row, (TOK, TOK)), 0.0), axis=1, keepdims=True
    )
    reach_row = norm_row * beta_row
    below = rows > cols
    strict = jnp.where(below, gram * norm_col * reach_row, 0.0)
    cross = jnp.where(below, nt(w0, key_rows) * norm_col, 0.0)
    unit = w0.astype(F32) * norm_col
    right = jnp.concatenate([unit, cross], axis=1)
    half = TOK // 2
    pl.semaphore_wait(barrier, len(near) + expected)
    values.x_begin(1)
    values.begin()
    inv_first, inv_second = inverse_pair(strict[:half, :half], strict[half:, half:])
    solved_first = mm3(inv_first, right[:half])
    solved_second = mm3(inv_second, right[half:] - mm3(strict[half:, :half], solved_first))
    solved = jnp.concatenate([solved_first, solved_second], axis=0)
    scaled_t = (unit * beta_col).T
    key_t = key_rows.astype(F32).T
    eye_head = (
        lax.broadcasted_iota(jnp.int32, (HEAD, HEAD), 0)
        == lax.broadcasted_iota(jnp.int32, (HEAD, HEAD), 1)
    ).astype(F32)
    own_map = jnp.concatenate([eye_head, key_t], axis=1) - mm3(scaled_t, solved)
    tkbuf[32 + inner] = own_map.astype(BF)
    solved_hi = solved.astype(BF)

    maps.x_begin(1)
    maps.begin()

    ones = jnp.ones((TOK, HEAD), BF)
    visible = rows >= cols
    lanes = lax.broadcasted_iota(jnp.int32, (TOK, HEAD), 1)
    first_lane = jnp.where(lanes == 0, 1.0, 0.0).astype(BF)

    own_values = jnp.concatenate([vbuf[32 + inner], ones], axis=1)

    def prepare_head(h, g, at):
        q = q_ref[:, pl.ds(pl.multiple_of(h * HEAD, HEAD), HEAD)]
        facing = jnp.where(visible, nt(q, w0) * reach_row, 0.0)
        face_hi = facing.astype(BF)
        moved = nn(face_hi, solved_hi)
        turned = (q.astype(F32) - moved[:, :HEAD]) * SCALE
        qext[g, at, :] = jnp.concatenate([turned.astype(BF), first_lane], axis=1)
        inside = (nt(q, key_rows) - moved[:, HEAD:]) * SCALE
        inside = jnp.where(visible, inside, NEG)
        peak = jnp.max(inside, axis=1, keepdims=True)
        weights = jnp.exp2(inside - peak).astype(BF)
        accs[g, at, :] = nn(weights, own_values)
        peaks[g, at, :] = jnp.broadcast_to(peak, (TOK, HEAD))

    def prepare_pair(g, carry):
        for half_pair in range(2):
            prepare_head(g * 2 + half_pair, g, slice(half_pair * TOK, half_pair * TOK + TOK))
        pl.when(g == 0)(lambda: values.after_z(0))
        pl.when(g == 1)(lambda: values.after_x(1))
        pl.when(g == 2)(lambda: maps.after_z(0))
        return carry

    lax.fori_loop(0, PAIRS, prepare_pair, 0)
    values.after_z(1)
    maps.after_x(1)
    maps.after_z(1)

    def forward(e):
        slot = 32 + inner - 2 * e

        @pl.when((slot % INNER // 4 != y) & (e < 16))
        def _():
            values.arrived(slot)
            maps.arrived(slot)

        @pl.when((e < 16) | (core == 1))
        def _():
            values.across(slot, e).start()
            maps.across(slot, e).start()

    def forward_step(e, carry):
        forward(e)
        return carry

    lax.fori_loop(1, AHEAD + 3, forward_step, 0)

    keyst[128:, :] = jnp.zeros((128, keyst.shape[1]), BF)
    tile_row = lax.broadcasted_iota(jnp.int32, (16, TOK), 0)
    chain[...] = eye_head
    own_doc = doc_ref[block]

    def carry_keys(index):
        distance = jnp.minimum(index + 1, SOURCES - 1)
        hi, lo = split(chain[...])
        both = tkbuf[32 + inner - distance]
        moved = nn(hi, both)
        chain[...] = moved[:, :HEAD] + nn(lo, both[:, :HEAD])
        at = pl.ds(pl.multiple_of(index * TOK, TOK), TOK)
        keyst[:HEAD, at] = moved[:, HEAD:].astype(BF)
        source = block - distance
        wanted = (
            (source >= 0) & (index < SOURCES - 1) & (doc_ref[jnp.maximum(source, 0)] == own_doc)
        )
        bias = jnp.where(wanted, 0.0, NEG)
        keyst[128:144, at] = jnp.where(tile_row == 0, bias, 0.0).astype(BF)
        vext[at, :] = jnp.concatenate([vbuf[32 + inner - distance], ones], axis=1)

    def odd_arrived(distance):
        slot = 32 + inner - distance
        values.arrived(slot)
        maps.arrived(slot)

    def first_keys(step, carry):
        odd_arrived(2 * step + 1)
        carry_keys(2 * step)
        carry_keys(2 * step + 1)
        return carry

    lax.fori_loop(0, CHUNK // 2, first_keys, 0)

    def produce(step, scores, highest):
        chunk = jnp.minimum(step // PAIRS, SOURCES // CHUNK - 1)
        at = pl.ds(pl.multiple_of(chunk * (CHUNK * TOK), TOK), CHUNK * TOK)
        made = nn(qext[step % PAIRS], keyst[:, at])
        scores[...] = made
        highest[...] = jnp.broadcast_to(jnp.max(made, axis=1, keepdims=True), highest.shape)

    def consume(step, scores, highest):
        g = step % PAIRS
        at = pl.ds(pl.multiple_of(step // PAIRS * (CHUNK * TOK), TOK), CHUNK * TOK)
        old = peaks[g]
        peak = jnp.maximum(old, highest[...])
        factor = jnp.exp2(old - peak)
        spread = jnp.concatenate([peak] * (CHUNK * TOK // HEAD), axis=1)
        weights = jnp.exp2(scores[...] - spread).astype(BF)
        accs[g] = accs[g] * jnp.concatenate([factor, factor], axis=1) + nn(weights, vext[at, :])
        peaks[g] = peak

    produce(0, score_a, high_a)

    def absorb(i, carry):
        pl.when(i == 0)(lambda: values.after_x(2))
        pl.when(i == 1)(lambda: values.after_z(2))
        pl.when(i == 1)(lambda: maps.after_x(2))
        pl.when(i == 3)(lambda: maps.after_z(2))
        pl.when(i + AHEAD + 3 <= 16)(lambda: forward(i + AHEAD + 3))
        pl.when(i < 14)(lambda: odd_arrived(2 * i + 5))
        produce(2 * i + 1, score_b, high_b)
        carry_keys(2 * i + 4)
        consume(2 * i, score_a, high_a)
        carry_keys(2 * i + 5)
        produce(2 * i + 2, score_a, high_a)
        consume(2 * i + 1, score_b, high_b)
        return carry

    lax.fori_loop(0, SOURCES // CHUNK * PAIRS // 2, absorb, 0)

    def finish(g, carry):
        for half_pair in range(2):
            total = accs[g, half_pair * TOK : half_pair * TOK + TOK, :]
            at = pl.ds(pl.multiple_of((g * 2 + half_pair) * HEAD, HEAD), HEAD)
            out_ref[:, at] = (total[:, :HEAD] / total[:, HEAD:]).astype(BF)
        return carry

    lax.fori_loop(0, PAIRS, finish, 0)
    values.drain()
    maps.drain()
    for mover in (values, maps):
        for e in range(17):
            when = {0: core == 0, 16: core == 1}.get(e)
            guarded(when, mover.across(32 + inner - 2 * e, e).wait_send)


def local(queries, keys, values, reflect, reflect_logit, doc_of_block):
    vmem = pl.BlockSpec(memory_space=pltpu.VMEM)
    return pl.pallas_call(
        kernel,
        out_shape=jax.ShapeDtypeStruct(queries.shape, BF),
        in_specs=[pl.BlockSpec(memory_space=pltpu.HBM)] * 6,
        out_specs=vmem,
        scratch_shapes=[
            pltpu.VMEM((TOK, HEADS * HEAD), BF),
            pltpu.VMEM((TOK, HEAD), BF),
            pltpu.VMEM((TOK, HEAD), BF),
            pltpu.VMEM((1, TOK), F32),
            pltpu.SMEM((256,), jnp.int32),
            pltpu.VMEM((SLOTS, TOK, HEAD), BF),
            pltpu.VMEM((SLOTS, HEAD, HEAD + TOK), BF),
            pltpu.VMEM((PAIRS, 2 * TOK, 2 * HEAD), BF),
            pltpu.VMEM((2 * HEAD, (SOURCES + CHUNK) * TOK), BF),
            pltpu.VMEM(((SOURCES + CHUNK) * TOK, 2 * HEAD), BF),
            pltpu.VMEM((PAIRS, 2 * TOK, 2 * HEAD), F32),
            pltpu.VMEM((PAIRS, 2 * TOK, HEAD), F32),
            pltpu.VMEM((HEAD, HEAD), F32),
            pltpu.VMEM((2 * TOK, CHUNK * TOK), F32),
            pltpu.VMEM((2 * TOK, CHUNK * TOK), F32),
            pltpu.VMEM((2 * TOK, HEAD), F32),
            pltpu.VMEM((2 * TOK, HEAD), F32),
            pltpu.SemaphoreType.DMA((SLOTS,)),
            pltpu.SemaphoreType.DMA((SLOTS,)),
            pltpu.SemaphoreType.DMA((SENDS + 17,)),
            pltpu.SemaphoreType.DMA((SENDS + 17,)),
            pltpu.SemaphoreType.DMA((6,)),
        ],
        compiler_params=pltpu.CompilerParams(
            collective_id=0, has_side_effects=True, vmem_limit_bytes=63 * 1024 * 1024
        ),
    )(queries, keys, values, reflect, reflect_logit.reshape(1, TOK), doc_of_block)


def solution(mesh):
    placed = (
        P(("outer", "inner"), None),
        P(("outer", "inner"), None),
        P(("outer", "inner"), None),
        P(("outer", "inner"), None),
        P(("outer", "inner")),
        P(),
    )
    return jax.shard_map(
        local, mesh=mesh, in_specs=placed, out_specs=P(("outer", "inner"), None), check_vma=False
    )
```
